512 devices in a mesh: section: 4 (over x), trial: 128 (over z, y, core).
Axes of the slice: x: 4, y: 4, z: 16, core: 2. Of those that a mesh axis runs over, the one named last changes fastest.
Arguments:
- spike_rates: bfloat16 [512, 256, 256], P(None, 'trial'), may hold values from -6 to 6
- first_preactivation: bfloat16 [1024, 256, 256], P('section', 'trial'), may hold values from -6 to 6
- second_preactivation: bfloat16 [1024, 256, 256], P('section', 'trial'), may hold values from -6 to 6
- output_gradient: bfloat16 [1024, 256, 256], P('section', 'trial'), may hold values from -0.29882812 to 0.29882812
- first_kernel: bfloat16 [3, 1024, 1024], P(None, None, 'section'), may hold values from -0.109375 to 0.109375
- second_kernel: bfloat16 [3, 1024, 1024], P(None, None, 'section'), may hold values from -0.109375 to 0.109375
- session_of: int32 [256], P('trial'), may hold values from 0 to 127, never falling along the last dimension, each value on 1 to 6 neighbouring positions
Outputs:
- readin_grad: bfloat16 [128, 512, 1024], P(None, 'trial', 'section')
The draws below stay inside these ranges and needn't reach their ends.
Inputs may be any that keep to these rules, and one draw needn't show every extreme that they name: `session_of`: the trials of a session are consecutive; every session has 1 to 6 trials, and one has exactly 6.
All inputs are finite; a program needn't handle non-finite values.
Results may differ from the reference program's by a relative error of at most 0.017.
Values may be sent and summed in bfloat16 or wider, within the bound.
No kernel may reach another device: no remote copies, remote signals or barrier semaphores. Data moves between devices by JAX's collectives and lax.ppermute only.
A program may use at most 64 MiB of HBM per device.

```python
import math
import jax
import jax.numpy as jnp
import numpy as np
from jax import lax

C = 1024
NEUR = 512
L = 256
FIRST_DILATION = 32
SECOND_DILATION = 64
TRIALS = 256
SESSIONS = 128
MOST = 6


def levels(own_key, extent, split, smallest, high):
    factor_of, own = 1.0, jax.random.fold_in(own_key, 6)
    for dim, blocks in split:
        draws = jnp.exp(jax.random.uniform(jax.random.fold_in(own, dim), (blocks,), jnp.float32, smallest / len(split), high / len(split)))
        factor_of = factor_of * jnp.repeat(draws, extent[dim] // blocks).reshape([-1 if axis == dim else 1 for axis in range(len(extent))])
    return factor_of


def length_profile(number_of, total, bound, slope):
    loads = [(1 << 20) // math.isqrt(grade ** slope) + 1 for grade in range(2, number_of + 1)]
    rest, holding = total - bound - (number_of - 1), [1] * (number_of - 1)
    while rest > 0:
        candidates = [i for i in range(number_of - 1) if holding[i] < bound]
        mass, left = sum([loads[i] for i in candidates]), rest
        for i in candidates:
            addition = min(bound - holding[i], max(1, left * loads[i] // mass), rest)
            holding[i] = holding[i] + addition
            rest = rest - addition
    return np.array([bound] + holding)


def uneven_parts(own_key, amount, total, reach, slope):
    if amount == 2:
        one = jax.random.randint(own_key, (), max(1, total - reach), min(reach, total - 1) + 1)
        return jnp.stack([one, total - one])
    tallies = jnp.asarray(length_profile(amount, total, reach, slope), jnp.int32)
    couples = (amount - 1) // 2
    source_of, taker = tallies[1:1 + 2 * couples:2], tallies[2:2 + 2 * couples:2]
    room = jnp.minimum(source_of - 1, reach - taker)
    moved = jax.random.randint(jax.random.fold_in(own_key, 1), (couples,), 0, 1 << 20) % (room + 1)
    tallies = tallies.at[1:1 + 2 * couples:2].set(source_of - moved).at[2:2 + 2 * couples:2].set(taker + moved)
    return tallies[jax.random.permutation(jax.random.fold_in(own_key, 2), amount)]


def scatter_about(rng, shape, width, bound, pieces=(), kind=jnp.bfloat16):
    drawn = width * jax.random.normal(rng, shape, jnp.float32)
    if pieces:
        drawn = drawn * levels(rng, shape, pieces, -0.22, 0.18)
    return jnp.clip(drawn, -bound, bound).astype(kind)


def setup_inputs(seed: int = 0) -> dict:
    keys = jax.random.split(jax.random.key(seed), 8)
    spike_rates = scatter_about(keys[0], (NEUR, TRIALS, L), 1.0, 6.0, ((1, 128),))
    first_preactivation = scatter_about(keys[1], (C, TRIALS, L), 1.0, 6.0, ((0, 4), (1, 128)))
    second_preactivation = scatter_about(keys[2], (C, TRIALS, L), 1.0, 6.0, ((0, 4), (1, 128)))
    output_gradient = scatter_about(keys[3], (C, TRIALS, L), 0.05, 0.29882812, ((0, 4), (1, 128)))
    first_kernel = scatter_about(keys[4], (3, C, C), (3 * C) ** -0.5, 0.109375, ((2, 4),))
    second_kernel = scatter_about(keys[5], (3, C, C), (3 * C) ** -0.5, 0.109375, ((2, 4),))
    session_of = jnp.searchsorted(jnp.cumsum(uneven_parts(keys[6], SESSIONS, TRIALS, MOST, 2)), jnp.arange(TRIALS), side="right").astype(jnp.int32)
    return {"spike_rates": spike_rates, "first_preactivation": first_preactivation, "second_preactivation": second_preactivation, "output_gradient": output_gradient, "first_kernel": first_kernel, "second_kernel": second_kernel, "session_of": session_of}


def gelu_slope(preact):
    values = preact.astype(jnp.float32)
    normal_cdf = 0.5 * (1.0 + lax.erf(values * (1.0 / math.sqrt(2.0))))
    density = jnp.exp(-0.5 * values * values) * (1.0 / math.sqrt(2.0 * math.pi))
    return normal_cdf + values * density

def shift_ahead(values, offset):
    padding = [(0, 0)] * (values.ndim - 1) + [(0, offset)]
    return jnp.pad(values[..., offset:], padding)

def conv_back(weights, flow_grad, spacing):
    flow_wide = flow_grad.astype(jnp.float32)
    running = None
    for kernel_tap in range(3):
        term_tap = jnp.einsum('co,oil->cil', weights[kernel_tap].astype(jnp.float32), flow_wide, precision=lax.Precision.HIGHEST)
        if kernel_tap > 0:
            term_tap = shift_ahead(term_tap, kernel_tap * spacing)
        running = term_tap if running is None else running + term_tap
    return running

def layer_backprop(upstream, preact, weights, spacing):
    flow_grad = (upstream.astype(jnp.float32) * gelu_slope(preact)).astype(jnp.bfloat16)
    return (upstream.astype(jnp.float32) + conv_back(weights, flow_grad, spacing)).astype(jnp.bfloat16)

def reference(spike_rates, first_preactivation, second_preactivation, output_gradient, first_kernel, second_kernel, session_of):
    upstream_gradient = layer_backprop(output_gradient, second_preactivation, second_kernel, SECOND_DILATION)
    input_gradient = layer_backprop(upstream_gradient, first_preactivation, first_kernel, FIRST_DILATION)

    def add_trial(carry, index):
        sample = lax.dynamic_slice_in_dim(spike_rates, index, 1, 1)[:, 0, :].astype(jnp.float32)
        grad_trial = lax.dynamic_slice_in_dim(input_gradient, index, 1, 1)[:, 0, :].astype(jnp.float32)
        product = jnp.dot(sample, grad_trial.T, precision=lax.Precision.HIGHEST)
        owner = lax.dynamic_slice_in_dim(session_of, index, 1, 0)[0].astype(jnp.int32)
        current = lax.dynamic_slice_in_dim(carry, owner, 1, 0)
        carry = lax.dynamic_update_slice_in_dim(carry, current + product[None], owner, 0)
        return (carry, None)
    start_sums = jnp.zeros((SESSIONS, NEUR, C), jnp.float32)
    result, _ = lax.scan(add_trial, start_sums, jnp.arange(TRIALS, dtype=jnp.int32))
    return result.astype(jnp.bfloat16)
```

```python
import math

import jax
import jax.numpy as jnp
from jax import lax
from jax.sharding import PartitionSpec as P

FIRST_DILATION = 32
SECOND_DILATION = 64


def gelu_slope(preact):
    values = preact.astype(jnp.float32)
    normal_cdf = 0.5 * (1.0 + lax.erf(values * (1.0 / math.sqrt(2.0))))
    density = jnp.exp(-0.5 * values * values) * (1.0 / math.sqrt(2.0 * math.pi))
    return normal_cdf + values * density


def shift_ahead(values, offset):
    padding = [(0, 0)] * (values.ndim - 1) + [(0, offset)]
    return jnp.pad(values[..., offset:], padding)


def layer_backprop(upstream, preact, weights, spacing):
    trials, own, steps = upstream.shape
    flow = (upstream.astype(jnp.float32) * gelu_slope(preact)).astype(jnp.bfloat16)
    stacked = jnp.concatenate([flow] + [shift_ahead(flow, tap * spacing) for tap in (1, 2)], axis=1)
    wide = jnp.concatenate([weights[tap] for tap in range(3)], axis=1)
    partial = jnp.einsum("co,iot->cit", wide, stacked, preferred_element_type=jnp.float32)
    shards = lax.axis_size("section")
    partial = partial.astype(jnp.bfloat16).reshape(shards, own, trials, steps)
    arrived = lax.all_to_all(partial, "section", split_axis=0, concat_axis=0, tiled=True)
    back = jnp.sum(arrived.astype(jnp.float32), axis=0)
    return (upstream.astype(jnp.float32) + back.transpose(1, 0, 2)).astype(jnp.bfloat16)


def body(
    spike_rates,
    first_preactivation,
    second_preactivation,
    output_gradient,
    first_kernel,
    second_kernel,
    session_of,
):
    by_trial = lambda a: a.transpose(1, 0, 2)
    upper = layer_backprop(
        by_trial(output_gradient), by_trial(second_preactivation), second_kernel, SECOND_DILATION
    )
    input_gradient = layer_backprop(upper, by_trial(first_preactivation), first_kernel, FIRST_DILATION)
    shards = lax.axis_size("trial")
    neurons, trials, steps = spike_rates.shape
    own = input_gradient.shape[1]
    block = neurons // shards
    parts = jnp.einsum("nit,ict->nic", spike_rates, input_gradient, preferred_element_type=jnp.float32)
    parts = parts.astype(jnp.bfloat16).reshape(shards, block * trials, own)
    marks = jnp.broadcast_to(session_of.astype(jnp.bfloat16)[None, :, None], (shards, trials, own))
    arrived = lax.all_to_all(
        jnp.concatenate([parts, marks], axis=1), "trial", split_axis=0, concat_axis=0, tiled=True
    )
    ids = arrived[:, block * trials :, 0].astype(jnp.int32).reshape(1, -1)
    rows = arrived[:, : block * trials].reshape(shards, block, trials, own)
    sessions = lax.broadcasted_iota(jnp.int32, (shards, 1), 0)
    chosen = (ids == sessions).astype(jnp.bfloat16).reshape(shards, shards, trials)
    return jnp.einsum("sdi,dnic->snc", chosen, rows, preferred_element_type=jnp.float32).astype(
        jnp.bfloat16
    )


def solution(mesh):
    in_specs = (
        P(None, "trial", None),
        P("section", "trial", None),
        P("section", "trial", None),
        P("section", "trial", None),
        P(None, None, "section"),
        P(None, None, "section"),
        P("trial"),
    )
    out_specs = P(None, "trial", "section")
    return jax.shard_map(body, mesh=mesh, in_specs=in_specs, out_specs=out_specs, check_vma=False)
```

```python
import math

import jax
import jax.numpy as jnp
from jax import lax
from jax.sharding import PartitionSpec as P

FIRST_DILATION = 32
SECOND_DILATION = 64


def gelu_slope(preact):
    values = preact.astype(jnp.float32)
    normal_cdf = 0.5 * (1.0 + lax.erf(values * (1.0 / math.sqrt(2.0))))
    density = jnp.exp(-0.5 * values * values) * (1.0 / math.sqrt(2.0 * math.pi))
    return normal_cdf + values * density


def shift_ahead(values, offset):
    padding = [(0, 0)] * (values.ndim - 1) + [(0, offset)]
    return jnp.pad(values[..., offset:], padding)


def layer_backprop(upstream, preact, weights, spacing):
    trials, own, steps = upstream.shape
    flow = (upstream.astype(jnp.float32) * gelu_slope(preact)).astype(jnp.bfloat16)
    stacked = jnp.concatenate([flow] + [shift_ahead(flow, tap * spacing) for tap in (1, 2)], axis=1)
    wide = jnp.concatenate([weights[tap] for tap in range(3)], axis=1)
    partial = jnp.einsum("co,iot->cit", wide, stacked, preferred_element_type=jnp.float32)
    shards = lax.axis_size("section")
    partial = partial.astype(jnp.bfloat16).reshape(shards, own, trials, steps)
    arrived = lax.all_to_all(partial, "section", split_axis=0, concat_axis=0, tiled=True)
    back = jnp.sum(arrived.astype(jnp.float32), axis=0)
    return (upstream.astype(jnp.float32) + back.transpose(1, 0, 2)).astype(jnp.bfloat16)


def body(
    spike_rates,
    first_preactivation,
    second_preactivation,
    output_gradient,
    first_kernel,
    second_kernel,
    session_of,
):
    by_trial = lambda a: a.transpose(1, 0, 2)
    upper = layer_backprop(
        by_trial(output_gradient), by_trial(second_preactivation), second_kernel, SECOND_DILATION
    )
    input_gradient = layer_backprop(upper, by_trial(first_preactivation), first_kernel, FIRST_DILATION)
    shards = lax.axis_size("trial")
    neurons, trials, steps = spike_rates.shape
    own = input_gradient.shape[1]
    rows = neurons // shards * own // 128
    parts = jnp.einsum("nit,ict->nic", spike_rates, input_gradient, preferred_element_type=jnp.float32)
    parts = parts.astype(jnp.bfloat16).reshape(neurons, trials, own // 128, 128)
    parts = parts.transpose(0, 2, 1, 3).reshape(shards, rows, trials, 128)
    marks = jnp.broadcast_to(session_of.astype(jnp.bfloat16)[None, None, :, None], (shards, 1, trials, 128))
    arrived = lax.all_to_all(
        jnp.concatenate([parts, marks], axis=1), "trial", split_axis=0, concat_axis=0, tiled=True
    )
    ids = arrived[:, rows, :, 0].astype(jnp.int32)
    sessions = lax.broadcasted_iota(jnp.int32, (shards, 1, 1), 0)
    chosen = (ids[None] == sessions).astype(jnp.bfloat16)
    summed = jnp.einsum(
        "sdi,dmil->sml", chosen, arrived[:, :rows], preferred_element_type=jnp.float32
    )
    return summed.astype(jnp.bfloat16).reshape(shards, neurons // shards, own)


def solution(mesh):
    in_specs = (
        P(None, "trial", None),
        P("section", "trial", None),
        P("section", "trial", None),
        P("section", "trial", None),
        P(None, None, "section"),
        P(None, None, "section"),
        P("trial"),
    )
    out_specs = P(None, "trial", "section")
    return jax.shard_map(body, mesh=mesh, in_specs=in_specs, out_specs=out_specs, check_vma=False)
```

```python
import math

import jax
import jax.numpy as jnp
from jax import lax
from jax.experimental import pallas as pl
from jax.experimental.pallas import tpu as pltpu
from jax.sharding import PartitionSpec as P

FIRST_DILATION = 32
SECOND_DILATION = 64


def gelu_slope(preact):
    values = preact.astype(jnp.float32)
    normal_cdf = 0.5 * (1.0 + lax.erf(values * (1.0 / math.sqrt(2.0))))
    density = jnp.exp(-0.5 * values * values) * (1.0 / math.sqrt(2.0 * math.pi))
    return normal_cdf + values * density


def shift_ahead(values, offset):
    return jnp.concatenate(
        [values[:, offset:], jnp.zeros((values.shape[0], offset), values.dtype)], axis=1
    )


def stack_taps(flow, spacing):
    return jnp.concatenate([flow] + [shift_ahead(flow, tap * spacing) for tap in (1, 2)], axis=0)


def block_sums(weights_ref, out_ref, wide_ref, sums_ref, in_sem, out_sem, make_flows, spacing):
    shards, trials, block, _ = out_ref.shape
    loads = [
        pltpu.make_async_copy(
            weights_ref.at[:, pl.ds(s * block, block), :], wide_ref.at[s], in_sem.at[s]
        )
        for s in range(shards)
    ]
    stores = [
        pltpu.make_async_copy(sums_ref.at[s], out_ref.at[s], out_sem.at[s]) for s in range(shards)
    ]
    for load in loads:
        load.start()
    stacked = [stack_taps(flow, spacing) for flow in make_flows()]
    for s in range(shards):
        loads[s].wait()
        wide = jnp.concatenate([wide_ref[s, tap] for tap in range(3)], axis=1)
        for trial in range(trials):
            total = jnp.dot(wide, stacked[trial], preferred_element_type=jnp.float32)
            sums_ref[s, trial] = total.astype(sums_ref.dtype)
        stores[s].start()
    for store in stores:
        store.wait()


def second_section(grad_ref, preact_ref, weights_ref, out_ref, *scratch):
    def make_flows():
        return [
            (grad_ref[trial].astype(jnp.float32) * gelu_slope(preact_ref[trial])).astype(jnp.bfloat16)
            for trial in range(grad_ref.shape[0])
        ]

    block_sums(weights_ref, out_ref, *scratch, make_flows, SECOND_DILATION)


def first_section(arrived_ref, grad_ref, preact_ref, weights_ref, out_ref, upper_ref, *scratch):
    def make_flows():
        flows = []
        for trial in range(grad_ref.shape[0]):
            back = arrived_ref[0, trial].astype(jnp.float32)
            for shard in range(1, arrived_ref.shape[0]):
                back = back + arrived_ref[shard, trial].astype(jnp.float32)
            upper = (grad_ref[trial].astype(jnp.float32) + back).astype(jnp.bfloat16)
            upper_ref[trial] = upper
            flows.append((upper.astype(jnp.float32) * preact_ref[trial]).astype(jnp.bfloat16))
        return flows

    block_sums(weights_ref, out_ref, *scratch, make_flows, FIRST_DILATION)


def body(
    spike_rates,
    first_preactivation,
    second_preactivation,
    output_gradient,
    first_kernel,
    second_kernel,
    session_of,
):
    sections, shards = lax.axis_size("section"), lax.axis_size("trial")
    neurons, trials, steps = spike_rates.shape
    own = output_gradient.shape[0]
    channels = first_kernel.shape[1]
    block = neurons // shards
    rows = block * own // 128

    near = pl.BlockSpec(memory_space=pltpu.VMEM)
    far = pl.BlockSpec(memory_space=pltpu.HBM)
    sums_shape = pltpu.HBM((sections, trials, own, steps), jnp.bfloat16)
    upper_shape = jax.ShapeDtypeStruct((trials, own, steps), jnp.bfloat16)
    scratch = [
        pltpu.VMEM((sections, 3, own, own), jnp.bfloat16),
        pltpu.VMEM((sections, trials, own, steps), jnp.bfloat16),
        pltpu.SemaphoreType.DMA((sections,)),
        pltpu.SemaphoreType.DMA((sections,)),
    ]
    params = pltpu.CompilerParams(vmem_limit_bytes=24 * 2**20)
    cost = pl.CostEstimate(
        flops=6 * channels * own * trials * steps,
        bytes_accessed=2 * (3 * channels * own + channels * trials * steps),
        transcendentals=2 * own * trials * steps,
    )

    def exchange(partial):
        return lax.all_to_all(partial, "section", split_axis=0, concat_axis=0, tiled=True)

    grad, first, second = (
        values.transpose(1, 0, 2)
        for values in (output_gradient, first_preactivation, second_preactivation)
    )
    partial = pl.pallas_call(
        second_section,
        in_specs=[near, near, far],
        out_specs=far,
        out_shape=sums_shape,
        scratch_shapes=scratch,
        compiler_params=params,
        cost_estimate=cost,
        name="second_section",
    )(grad, second, pltpu.with_memory_space_constraint(second_kernel, pltpu.HBM))
    place = lax.broadcasted_iota(jnp.int32, (shards, trials), 0)
    ids = jnp.where(place == lax.axis_index("trial"), session_of[None, :], 0).reshape(-1, 128)
    span, layer = shards // 4, 8
    layers = [[start + j for j in range(layer)] for start in range(0, shards, layer)]
    columns = [
        [start + side + j for j in range(0, span, layer)]
        for start in range(0, shards, span)
        for side in range(layer)
    ]
    ids = lax.optimization_barrier((ids, partial))[0]
    ids = lax.psum(ids, "trial", axis_index_groups=layers)
    arrived, ids = lax.optimization_barrier((exchange(partial), ids))
    partial, upper = pl.pallas_call(
        first_section,
        in_specs=[near, near, near, far],
        out_specs=[far, near],
        out_shape=[sums_shape, upper_shape],
        scratch_shapes=scratch,
        compiler_params=params,
        cost_estimate=cost,
        name="first_section",
    )(arrived, grad, gelu_slope(first), pltpu.with_memory_space_constraint(first_kernel, pltpu.HBM))
    ids = lax.optimization_barrier((ids, partial))[0]
    ids = lax.psum(ids, "trial", axis_index_groups=columns)
    arrived, ids = lax.optimization_barrier((exchange(partial), ids))
    ids = ids + sum(
        lax.ppermute(ids, "trial", [(j, (j + k * span) % shards) for j in range(shards)])
        for k in (2, 1, 3)
    )
    moved = jnp.sum(arrived.astype(jnp.float32), axis=0)
    input_gradient = (upper.astype(jnp.float32) + moved).astype(jnp.bfloat16)

    parts = jnp.einsum("nit,ict->nic", spike_rates, input_gradient, preferred_element_type=jnp.float32)
    parts = parts.astype(jnp.bfloat16).reshape(shards, block * trials, own)
    arrived = lax.all_to_all(parts, "trial", split_axis=0, concat_axis=0, tiled=True)
    keys = ids.reshape(shards, 1, trials) * block + lax.broadcasted_iota(jnp.int32, (1, block, 1), 1)
    slots = lax.broadcasted_iota(jnp.int32, (shards * block, 1), 0)
    chosen = (keys.reshape(1, -1) == slots).astype(jnp.bfloat16)
    summed = jnp.dot(chosen, arrived.reshape(-1, own), preferred_element_type=jnp.float32)
    return summed.astype(jnp.bfloat16).reshape(shards, block, own)


def solution(mesh):
    in_specs = (
        P(None, "trial", None),
        P("section", "trial", None),
        P("section", "trial", None),
        P("section", "trial", None),
        P(None, None, "section"),
        P(None, None, "section"),
        P("trial"),
    )
    out_specs = P(None, "trial", "section")
    return jax.shard_map(body, mesh=mesh, in_specs=in_specs, out_specs=out_specs, check_vma=False)
```

```python
import math

import jax
import jax.numpy as jnp
from jax import lax
from jax.experimental import pallas as pl
from jax.experimental.pallas import tpu as pltpu
from jax.sharding import PartitionSpec as P

FIRST_DILATION = 32
SECOND_DILATION = 64


def gelu_slope(preact):
    values = preact.astype(jnp.float32)
    normal_cdf = 0.5 * (1.0 + lax.erf(values * (1.0 / math.sqrt(2.0))))
    density = jnp.exp(-0.5 * values * values) * (1.0 / math.sqrt(2.0 * math.pi))
    return normal_cdf + values * density


def shift_ahead(values, offset):
    return jnp.concatenate(
        [values[:, offset:], jnp.zeros((values.shape[0], offset), values.dtype)], axis=1
    )


def stack_taps(flow, spacing):
    return jnp.concatenate([flow] + [shift_ahead(flow, tap * spacing) for tap in (1, 2)], axis=0)


def weight_loads(weights_ref, wide_ref, in_sem, first=0):
    count, taps, block, _ = wide_ref.shape
    return [
        pltpu.make_async_copy(
            weights_ref.at[tap, pl.ds((first + s) * block, block), :],
            wide_ref.at[s, tap],
            in_sem.at[s, tap],
        )
        for s in range(count)
        for tap in range(taps)
    ]


def fetch(weights_ref, after_ref, wide_ref, in_sem):
    loads = weight_loads(weights_ref, wide_ref, in_sem)
    for load in loads:
        load.start()
    for load in loads:
        load.wait()


def take_weights(early_ref, wide_ref, loads, s, block):
    if wide_ref is None:
        return [early_ref[tap, s * block : (s + 1) * block, :] for tap in range(early_ref.shape[0])]
    early, taps = early_ref.shape[:2]
    if s < early:
        return [early_ref[s, tap] for tap in range(taps)]
    for load in loads[taps * (s - early) : taps * (s - early + 1)]:
        load.wait()
    return [wide_ref[s - early, tap] for tap in range(taps)]


def block_sums(early_ref, wide_ref, loads, out_ref, sums_ref, out_sem, flows, spacing):
    shards, trials, block, _ = out_ref.shape
    stores = [
        pltpu.make_async_copy(sums_ref.at[s], out_ref.at[s], out_sem.at[s]) for s in range(shards)
    ]
    stacked = [stack_taps(flow, spacing) for flow in flows]
    for s in range(shards):
        wide = jnp.concatenate(take_weights(early_ref, wide_ref, loads, s, block), axis=1)
        for trial in range(trials):
            total = jnp.dot(wide, stacked[trial], preferred_element_type=jnp.float32)
            sums_ref[s, trial] = total.astype(sums_ref.dtype)
        stores[s].start()
    for store in stores:
        store.wait()


def second_section(grad_ref, preact_ref, weights_ref, out_ref, sums_ref, out_sem):
    flows = [
        (grad_ref[trial].astype(jnp.float32) * gelu_slope(preact_ref[trial])).astype(jnp.bfloat16)
        for trial in range(grad_ref.shape[0])
    ]
    block_sums(weights_ref, None, [], out_ref, sums_ref, out_sem, flows, SECOND_DILATION)


def first_section(
    arrived_ref, grad_ref, slope_ref, early_ref, weights_ref, out_ref, upper_ref, sums_ref, out_sem, wide_ref, in_sem
):
    loads = weight_loads(weights_ref, wide_ref, in_sem, first=early_ref.shape[0])
    for load in loads:
        load.start()
    flows = []
    for trial in range(grad_ref.shape[0]):
        back = arrived_ref[0, trial].astype(jnp.float32)
        for shard in range(1, arrived_ref.shape[0]):
            back = back + arrived_ref[shard, trial].astype(jnp.float32)
        upper = (grad_ref[trial].astype(jnp.float32) + back).astype(jnp.bfloat16)
        upper_ref[trial] = upper
        flows.append((upper.astype(jnp.float32) * slope_ref[trial]).astype(jnp.bfloat16))
    block_sums(early_ref, wide_ref, loads, out_ref, sums_ref, out_sem, flows, FIRST_DILATION)


def readin(arrived_ref, upper_ref, spikes_ref, out_ref, parts_ref, out_sem):
    shards, trials, own, _ = arrived_ref.shape
    gradients = []
    for trial in range(trials):
        total = upper_ref[trial].astype(jnp.float32)
        for shard in range(shards):
            total = total + arrived_ref[shard, trial].astype(jnp.float32)
        gradients.append(total.astype(jnp.bfloat16))
    joined = jnp.concatenate(gradients, axis=0)
    chunks, rows, _ = parts_ref.shape
    trial_of_row = lax.rem(lax.broadcasted_iota(jnp.int32, (rows, own), 0), trials)
    stores = []
    for k in range(chunks):
        products = lax.dot_general(
            spikes_ref[k * rows : (k + 1) * rows, :],
            joined,
            (((1,), (1,)), ((), ())),
            preferred_element_type=jnp.float32,
        )
        picked = products[:, :own]
        for trial in range(1, trials):
            picked = jnp.where(
                trial_of_row == trial, products[:, trial * own : (trial + 1) * own], picked
            )
        parts_ref[k] = picked.astype(parts_ref.dtype)
        stores.append(
            pltpu.make_async_copy(
                parts_ref.at[k], out_ref.at[pl.ds(k * rows, rows), :], out_sem.at[k]
            )
        )
        stores[-1].start()
    for store in stores:
        store.wait()


def body(
    spike_rates,
    first_preactivation,
    second_preactivation,
    output_gradient,
    first_kernel,
    second_kernel,
    session_of,
):
    sections, shards = lax.axis_size("section"), lax.axis_size("trial")
    neurons, trials, steps = spike_rates.shape
    own = output_gradient.shape[0]
    channels = first_kernel.shape[1]
    block = neurons // shards
    rows = block * own // 128

    near = pl.BlockSpec(memory_space=pltpu.VMEM)
    far = pl.BlockSpec(memory_space=pltpu.HBM)
    sums_shape = pltpu.HBM((sections, trials, own, steps), jnp.bfloat16)
    upper_shape = jax.ShapeDtypeStruct((trials, own, steps), jnp.bfloat16)
    wide_shape = (sections, 3, own, own)
    scratch = [
        pltpu.VMEM((sections, trials, own, steps), jnp.bfloat16),
        pltpu.SemaphoreType.DMA((sections,)),
    ]
    params = pltpu.CompilerParams(vmem_limit_bytes=10 * 2**20)
    cost = pl.CostEstimate(
        flops=6 * channels * own * trials * steps,
        bytes_accessed=2 * (3 * channels * own + channels * trials * steps),
        transcendentals=2 * own * trials * steps,
    )

    def exchange(partial):
        return lax.all_to_all(partial, "section", split_axis=0, concat_axis=0, tiled=True)

    grad, first, second = (
        values.transpose(1, 0, 2)
        for values in (output_gradient, first_preactivation, second_preactivation)
    )
    partial = pl.pallas_call(
        second_section,
        in_specs=[near, near, near],
        out_specs=far,
        out_shape=sums_shape,
        scratch_shapes=scratch,
        compiler_params=params,
        cost_estimate=cost,
        name="second_section",
    )(grad, second, second_kernel)
    place = lax.broadcasted_iota(jnp.int32, (shards, trials), 0)
    ids = jnp.where(place == lax.axis_index("trial"), session_of[None, :], 0).reshape(-1, 128)
    span, layer = shards // 4, 8
    layers = [[start + j for j in range(layer)] for start in range(0, shards, layer)]
    columns = [
        [start + side + j for j in range(0, span, layer)]
        for start in range(0, shards, span)
        for side in range(layer)
    ]
    ids = lax.optimization_barrier((ids, partial))[0]
    ids = lax.psum(ids, "trial", axis_index_groups=layers)
    first_weights = pltpu.with_memory_space_constraint(first_kernel, pltpu.HBM)
    early_shape = (1, *wide_shape[1:])
    late_shape = (sections - 1, *wide_shape[1:])
    early = pl.pallas_call(
        fetch,
        in_specs=[far, pl.BlockSpec(memory_space=pl.ANY)],
        out_specs=near,
        out_shape=pltpu.VMEM(early_shape, jnp.bfloat16),
        scratch_shapes=[pltpu.SemaphoreType.DMA(early_shape[:2])],
        compiler_params=params,
        cost_estimate=pl.CostEstimate(
            flops=0, bytes_accessed=2 * first_kernel.size, transcendentals=0
        ),
        name="fetch_first_kernel",
    )(first_weights, ids)
    arrived, ids, early = lax.optimization_barrier((exchange(partial), ids, early))
    partial, upper = pl.pallas_call(
        first_section,
        in_specs=[near, near, near, near, far],
        out_specs=[far, near],
        out_shape=[sums_shape, upper_shape],
        scratch_shapes=scratch
        + [pltpu.VMEM(late_shape, jnp.bfloat16), pltpu.SemaphoreType.DMA(late_shape[:2])],
        compiler_params=params,
        cost_estimate=cost,
        name="first_section",
    )(arrived, grad, gelu_slope(first), early, first_weights)
    ids = lax.optimization_barrier((ids, partial))[0]
    ids = lax.psum(ids, "trial", axis_index_groups=columns)
    arrived, ids = lax.optimization_barrier((exchange(partial), ids))
    ids = ids + sum(
        lax.ppermute(ids, "trial", [(j, (j + k * span) % shards) for j in range(shards)])
        for k in (2, 1, 3)
    )
    flat_shape = (neurons * trials, steps)
    parts = pl.pallas_call(
        readin,
        in_specs=[near, near, near],
        out_specs=far,
        out_shape=pltpu.HBM((neurons * trials, own), jnp.bfloat16),
        scratch_shapes=[
            pltpu.VMEM((sections, neurons * trials // sections, own), jnp.bfloat16),
            pltpu.SemaphoreType.DMA((sections,)),
        ],
        compiler_params=params,
        cost_estimate=pl.CostEstimate(
            flops=2 * neurons * trials * trials * own * steps,
            bytes_accessed=4 * neurons * trials * own,
            transcendentals=0,
        ),
        name="readin",
    )(arrived, upper, spike_rates.reshape(flat_shape))
    parts = parts.reshape(shards, block * trials, own)
    arrived = lax.all_to_all(parts, "trial", split_axis=0, concat_axis=0, tiled=True)
    keys = ids.reshape(shards, 1, trials) * block + lax.broadcasted_iota(jnp.int32, (1, block, 1), 1)
    slots = lax.broadcasted_iota(jnp.int32, (shards * block, 1), 0)
    chosen = (keys.reshape(1, -1) == slots).astype(jnp.bfloat16)
    summed = jnp.dot(chosen, arrived.reshape(-1, own), preferred_element_type=jnp.float32)
    return summed.astype(jnp.bfloat16).reshape(shards, block, own)


def solution(mesh):
    in_specs = (
        P(None, "trial", None),
        P("section", "trial", None),
        P("section", "trial", None),
        P("section", "trial", None),
        P(None, None, "section"),
        P(None, None, "section"),
        P("trial"),
    )
    out_specs = P(None, "trial", "section")
    return jax.shard_map(body, mesh=mesh, in_specs=in_specs, out_specs=out_specs, check_vma=False)
```

```python
import math

import jax
import jax.numpy as jnp
from jax import lax
from jax.experimental import pallas as pl
from jax.experimental.pallas import tpu as pltpu
from jax.sharding import PartitionSpec as P

FIRST_DILATION = 32
SECOND_DILATION = 64


def gelu_slope(preact):
    values = preact.astype(jnp.float32)
    normal_cdf = 0.5 * (1.0 + lax.erf(values * (1.0 / math.sqrt(2.0))))
    density = jnp.exp(-0.5 * values * values) * (1.0 / math.sqrt(2.0 * math.pi))
    return normal_cdf + values * density


def shift_ahead(values, offset):
    return jnp.concatenate(
        [values[:, offset:], jnp.zeros((values.shape[0], offset), values.dtype)], axis=1
    )


def stack_taps(flow, spacing):
    return jnp.concatenate([flow] + [shift_ahead(flow, tap * spacing) for tap in (1, 2)], axis=0)


def weight_loads(weights_ref, wide_ref, in_sem, first=0):
    count, taps, block, _ = wide_ref.shape
    return [
        pltpu.make_async_copy(
            weights_ref.at[tap, pl.ds((first + s) * block, block), :],
            wide_ref.at[s, tap],
            in_sem.at[s, tap],
        )
        for s in range(count)
        for tap in range(taps)
    ]


def fetch(weights_ref, after_ref, wide_ref, in_sem):
    loads = weight_loads(weights_ref, wide_ref, in_sem)
    for load in loads:
        load.start()
    for load in loads:
        load.wait()


def block_sums(weights_of, out_ref, sums_ref, out_sem, flows, spacing):
    shards, trials, _, _ = out_ref.shape
    stores = [
        pltpu.make_async_copy(sums_ref.at[s], out_ref.at[s], out_sem.at[s]) for s in range(shards)
    ]
    stacked = [stack_taps(flow, spacing) for flow in flows]
    for s in range(shards):
        wide = jnp.concatenate(weights_of(s), axis=1)
        for trial in range(trials):
            total = jnp.dot(wide, stacked[trial], preferred_element_type=jnp.float32)
            sums_ref[s, trial] = total.astype(sums_ref.dtype)
        stores[s].start()
    for store in stores:
        store.wait()


def second_section(grad_ref, preact_ref, weights_ref, out_ref, sums_ref, out_sem):
    flows = [
        (grad_ref[trial].astype(jnp.float32) * gelu_slope(preact_ref[trial])).astype(jnp.bfloat16)
        for trial in range(grad_ref.shape[0])
    ]
    block = out_ref.shape[2]

    def weights_of(s):
        return [weights_ref[tap, s * block : (s + 1) * block, :] for tap in range(3)]

    block_sums(weights_of, out_ref, sums_ref, out_sem, flows, SECOND_DILATION)


def first_section(
    arrived_ref, grad_ref, preact_ref, wide_ref, out_ref, upper_ref, sums_ref, out_sem
):
    flows = []
    for trial in range(grad_ref.shape[0]):
        back = arrived_ref[0, trial].astype(jnp.float32)
        for shard in range(1, arrived_ref.shape[0]):
            back = back + arrived_ref[shard, trial].astype(jnp.float32)
        upper = (grad_ref[trial].astype(jnp.float32) + back).astype(jnp.bfloat16)
        upper_ref[trial] = upper
        slope = gelu_slope(preact_ref[trial])
        flows.append((upper.astype(jnp.float32) * slope).astype(jnp.bfloat16))

    def weights_of(s):
        return [wide_ref[s, tap] for tap in range(3)]

    block_sums(weights_of, out_ref, sums_ref, out_sem, flows, FIRST_DILATION)


def readin(arrived_ref, upper_ref, spikes_ref, out_ref, parts_ref, out_sem):
    shards, trials, own, _ = arrived_ref.shape
    gradients = []
    for trial in range(trials):
        total = upper_ref[trial].astype(jnp.float32)
        for shard in range(shards):
            total = total + arrived_ref[shard, trial].astype(jnp.float32)
        gradients.append(total.astype(jnp.bfloat16))
    joined = jnp.concatenate(gradients, axis=0)
    chunks, rows, _ = parts_ref.shape
    trial_of_row = lax.rem(lax.broadcasted_iota(jnp.int32, (rows, own), 0), trials)
    stores = []
    for k in range(chunks):
        products = lax.dot_general(
            spikes_ref[k * rows : (k + 1) * rows, :],
            joined,
            (((1,), (1,)), ((), ())),
            preferred_element_type=jnp.float32,
        )
        picked = products[:, :own]
        for trial in range(1, trials):
            picked = jnp.where(
                trial_of_row == trial, products[:, trial * own : (trial + 1) * own], picked
            )
        parts_ref[k] = picked.astype(parts_ref.dtype)
        stores.append(
            pltpu.make_async_copy(
                parts_ref.at[k], out_ref.at[pl.ds(k * rows, rows), :], out_sem.at[k]
            )
        )
        stores[-1].start()
    for store in stores:
        store.wait()


def body(
    spike_rates,
    first_preactivation,
    second_preactivation,
    output_gradient,
    first_kernel,
    second_kernel,
    session_of,
):
    sections, shards = lax.axis_size("section"), lax.axis_size("trial")
    neurons, trials, steps = spike_rates.shape
    own = output_gradient.shape[0]
    channels = first_kernel.shape[1]
    block = neurons // shards
    rows = block * own // 128

    near = pl.BlockSpec(memory_space=pltpu.VMEM)
    far = pl.BlockSpec(memory_space=pltpu.HBM)
    sums_shape = pltpu.HBM((sections, trials, own, steps), jnp.bfloat16)
    upper_shape = jax.ShapeDtypeStruct((trials, own, steps), jnp.bfloat16)
    wide_shape = (sections, 3, own, own)
    scratch = [
        pltpu.VMEM((sections, trials, own, steps), jnp.bfloat16),
        pltpu.SemaphoreType.DMA((sections,)),
    ]
    params = pltpu.CompilerParams(vmem_limit_bytes=10 * 2**20)
    cost = pl.CostEstimate(
        flops=6 * channels * own * trials * steps,
        bytes_accessed=2 * (3 * channels * own + channels * trials * steps),
        transcendentals=2 * own * trials * steps,
    )

    def exchange(partial):
        return lax.all_to_all(partial, "section", split_axis=0, concat_axis=0, tiled=True)

    grad, first, second = (
        values.transpose(1, 0, 2)
        for values in (output_gradient, first_preactivation, second_preactivation)
    )
    partial = pl.pallas_call(
        second_section,
        in_specs=[near, near, near],
        out_specs=far,
        out_shape=sums_shape,
        scratch_shapes=scratch,
        compiler_params=params,
        cost_estimate=cost,
        name="second_section",
    )(grad, second, second_kernel)
    place = lax.broadcasted_iota(jnp.int32, (shards, trials), 0)
    ids = jnp.where(place == lax.axis_index("trial"), session_of[None, :], 0).reshape(-1, 128)
    span, layer = shards // 4, 8
    layers = [[start + j for j in range(layer)] for start in range(0, shards, layer)]
    columns = [
        [start + side + j for j in range(0, span, layer)]
        for start in range(0, shards, span)
        for side in range(layer)
    ]
    quarters = [[start + j for j in range(0, shards, span)] for start in range(span)]
    ids = lax.optimization_barrier((ids, partial))[0]
    ids = lax.psum(ids, "trial", axis_index_groups=columns)
    first_weights = pltpu.with_memory_space_constraint(first_kernel, pltpu.HBM)
    early = pl.pallas_call(
        fetch,
        in_specs=[far, pl.BlockSpec(memory_space=pl.ANY)],
        out_specs=near,
        out_shape=pltpu.VMEM(wide_shape, jnp.bfloat16),
        scratch_shapes=[pltpu.SemaphoreType.DMA(wide_shape[:2])],
        compiler_params=params,
        cost_estimate=pl.CostEstimate(
            flops=0, bytes_accessed=2 * first_kernel.size, transcendentals=0
        ),
        name="fetch_first_kernel",
    )(first_weights, ids)
    arrived, ids, early = lax.optimization_barrier((exchange(partial), ids, early))
    partial, upper = pl.pallas_call(
        first_section,
        in_specs=[near, near, near, near],
        out_specs=[far, near],
        out_shape=[sums_shape, upper_shape],
        scratch_shapes=scratch,
        compiler_params=params,
        cost_estimate=cost,
        name="first_section",
    )(arrived, grad, first, early)
    ids = lax.optimization_barrier((ids, partial))[0]
    ids = lax.psum(ids, "trial", axis_index_groups=quarters)
    arrived, ids = lax.optimization_barrier((exchange(partial), ids))
    flat_shape = (neurons * trials, steps)
    parts = pl.pallas_call(
        readin,
        in_specs=[near, near, near],
        out_specs=far,
        out_shape=pltpu.HBM((neurons * trials, own), jnp.bfloat16),
        scratch_shapes=[
            pltpu.VMEM((sections, neurons * trials // sections, own), jnp.bfloat16),
            pltpu.SemaphoreType.DMA((sections,)),
        ],
        compiler_params=params,
        cost_estimate=pl.CostEstimate(
            flops=2 * neurons * trials * trials * own * steps,
            bytes_accessed=4 * neurons * trials * own,
            transcendentals=0,
        ),
        name="readin",
    )(arrived, upper, spike_rates.reshape(flat_shape))
    parts = parts.reshape(shards, block * trials, own)
    arrived = lax.all_to_all(parts, "trial", split_axis=0, concat_axis=0, tiled=True)
    ids = lax.optimization_barrier((ids, parts))[0]
    ids = lax.psum(ids, "trial", axis_index_groups=layers)
    keys = ids.reshape(shards, 1, trials) * block + lax.broadcasted_iota(jnp.int32, (1, block, 1), 1)
    slots = lax.broadcasted_iota(jnp.int32, (shards * block, 1), 0)
    chosen = (keys.reshape(1, -1) == slots).astype(jnp.bfloat16)
    summed = jnp.dot(chosen, arrived.reshape(-1, own), preferred_element_type=jnp.float32)
    return summed.astype(jnp.bfloat16).reshape(shards, block, own)


def solution(mesh):
    in_specs = (
        P(None, "trial", None),
        P("section", "trial", None),
        P("section", "trial", None),
        P("section", "trial", None),
        P(None, None, "section"),
        P(None, None, "section"),
        P("trial"),
    )
    out_specs = P(None, "trial", "section")
    return jax.shard_map(body, mesh=mesh, in_specs=in_specs, out_specs=out_specs, check_vma=False)
```

```python
import math

import jax
import jax.numpy as jnp
from jax import lax
from jax.experimental import pallas as pl
from jax.experimental.pallas import tpu as pltpu
from jax.sharding import PartitionSpec as P

FIRST_DILATION = 32
SECOND_DILATION = 64


def gelu_slope(preact):
    values = preact.astype(jnp.float32)
    normal_cdf = 0.5 * (1.0 + lax.erf(values * (1.0 / math.sqrt(2.0))))
    density = jnp.exp(-0.5 * values * values) * (1.0 / math.sqrt(2.0 * math.pi))
    return normal_cdf + values * density


def shift_ahead(values, offset):
    return jnp.concatenate(
        [values[:, offset:], jnp.zeros((values.shape[0], offset), values.dtype)], axis=1
    )


def stack_taps(flow, spacing):
    return jnp.concatenate([flow] + [shift_ahead(flow, tap * spacing) for tap in (1, 2)], axis=0)


def weight_loads(weights_ref, wide_ref, in_sem, first=0):
    count, taps, block, _ = wide_ref.shape
    return [
        pltpu.make_async_copy(
            weights_ref.at[tap, pl.ds((first + s) * block, block), :],
            wide_ref.at[s, tap],
            in_sem.at[s, tap],
        )
        for s in range(count)
        for tap in range(taps)
    ]


def fetch(weights_ref, after_ref, wide_ref, in_sem):
    loads = weight_loads(weights_ref, wide_ref, in_sem)
    for load in loads:
        load.start()
    for load in loads:
        load.wait()


def block_sums(weights_of, out_ref, sums_ref, out_sem, flows, spacing):
    shards, trials, _, _ = out_ref.shape
    stores = [
        pltpu.make_async_copy(sums_ref.at[s], out_ref.at[s], out_sem.at[s]) for s in range(shards)
    ]
    stacked = [stack_taps(flow, spacing) for flow in flows]
    for s in range(shards):
        wide = jnp.concatenate(weights_of(s), axis=1)
        for trial in range(trials):
            total = jnp.dot(wide, stacked[trial], preferred_element_type=jnp.float32)
            sums_ref[s, trial] = total.astype(sums_ref.dtype)
        stores[s].start()
    for store in stores:
        store.wait()


def second_section(grad_ref, preact_ref, weights_ref, out_ref, sums_ref, out_sem):
    flows = [
        (grad_ref[trial].astype(jnp.float32) * gelu_slope(preact_ref[trial])).astype(jnp.bfloat16)
        for trial in range(grad_ref.shape[0])
    ]
    block = out_ref.shape[2]

    def weights_of(s):
        return [weights_ref[tap, s * block : (s + 1) * block, :] for tap in range(3)]

    block_sums(weights_of, out_ref, sums_ref, out_sem, flows, SECOND_DILATION)


def first_section(
    arrived_ref, grad_ref, preact_ref, wide_ref, out_ref, upper_ref, sums_ref, out_sem
):
    flows = []
    for trial in range(grad_ref.shape[0]):
        back = arrived_ref[0, trial].astype(jnp.float32)
        for shard in range(1, arrived_ref.shape[0]):
            back = back + arrived_ref[shard, trial].astype(jnp.float32)
        upper = (grad_ref[trial].astype(jnp.float32) + back).astype(jnp.bfloat16)
        upper_ref[trial] = upper
        slope = gelu_slope(preact_ref[trial])
        flows.append((upper.astype(jnp.float32) * slope).astype(jnp.bfloat16))

    def weights_of(s):
        return [wide_ref[s, tap] for tap in range(3)]

    block_sums(weights_of, out_ref, sums_ref, out_sem, flows, FIRST_DILATION)


def readin(arrived_ref, upper_ref, spikes_ref, out_ref, parts_ref, out_sem):
    shards, trials, own, _ = arrived_ref.shape
    gradients = []
    for trial in range(trials):
        total = upper_ref[trial].astype(jnp.float32)
        for shard in range(shards):
            total = total + arrived_ref[shard, trial].astype(jnp.float32)
        gradients.append(total.astype(jnp.bfloat16))
    joined = jnp.concatenate(gradients, axis=0)
    chunks, rows, _ = parts_ref.shape
    trial_of_row = lax.rem(lax.broadcasted_iota(jnp.int32, (rows, own), 0), trials)
    stores = []
    for k in range(chunks):
        products = lax.dot_general(
            spikes_ref[k * rows : (k + 1) * rows, :],
            joined,
            (((1,), (1,)), ((), ())),
            preferred_element_type=jnp.float32,
        )
        picked = products[:, :own]
        for trial in range(1, trials):
            picked = jnp.where(
                trial_of_row == trial, products[:, trial * own : (trial + 1) * own], picked
            )
        parts_ref[k] = picked.astype(parts_ref.dtype)
        stores.append(
            pltpu.make_async_copy(
                parts_ref.at[k], out_ref.at[pl.ds(k * rows, rows), :], out_sem.at[k]
            )
        )
        stores[-1].start()
    for store in stores:
        store.wait()


def body(
    spike_rates,
    first_preactivation,
    second_preactivation,
    output_gradient,
    first_kernel,
    second_kernel,
    session_of,
):
    sections, shards = lax.axis_size("section"), lax.axis_size("trial")
    neurons, trials, steps = spike_rates.shape
    own = output_gradient.shape[0]
    channels = first_kernel.shape[1]
    block = neurons // shards
    rows = block * own // 128

    near = pl.BlockSpec(memory_space=pltpu.VMEM)
    far = pl.BlockSpec(memory_space=pltpu.HBM)
    sums_shape = pltpu.HBM((sections, trials, own, steps), jnp.bfloat16)
    upper_shape = jax.ShapeDtypeStruct((trials, own, steps), jnp.bfloat16)
    wide_shape = (sections, 3, own, own)
    scratch = [
        pltpu.VMEM((sections, trials, own, steps), jnp.bfloat16),
        pltpu.SemaphoreType.DMA((sections,)),
    ]
    params = pltpu.CompilerParams(vmem_limit_bytes=10 * 2**20)
    cost = pl.CostEstimate(
        flops=6 * channels * own * trials * steps,
        bytes_accessed=2 * (3 * channels * own + channels * trials * steps),
        transcendentals=2 * own * trials * steps,
    )

    def exchange(partial):
        return lax.all_to_all(partial, "section", split_axis=0, concat_axis=0, tiled=True)

    grad, first, second = (
        values.transpose(1, 0, 2)
        for values in (output_gradient, first_preactivation, second_preactivation)
    )
    partial = pl.pallas_call(
        second_section,
        in_specs=[near, near, near],
        out_specs=far,
        out_shape=sums_shape,
        scratch_shapes=scratch,
        compiler_params=params,
        cost_estimate=cost,
        name="second_section",
    )(grad, second, second_kernel)
    place = lax.broadcasted_iota(jnp.int32, (shards, trials), 0)
    ids = jnp.where(place == lax.axis_index("trial"), session_of[None, :], 0).reshape(-1, 128)
    span = shards // 4
    neighbours = [[start + j for j in range(span)] for start in range(0, shards, span)]
    quarters = [[start + j for j in range(0, shards, span)] for start in range(span)]
    ids = lax.optimization_barrier((ids, partial))[0]
    first_weights = pltpu.with_memory_space_constraint(first_kernel, pltpu.HBM)
    early = pl.pallas_call(
        fetch,
        in_specs=[far, pl.BlockSpec(memory_space=pl.ANY)],
        out_specs=near,
        out_shape=pltpu.VMEM(wide_shape, jnp.bfloat16),
        scratch_shapes=[pltpu.SemaphoreType.DMA(wide_shape[:2])],
        compiler_params=params,
        cost_estimate=pl.CostEstimate(
            flops=0, bytes_accessed=2 * first_kernel.size, transcendentals=0
        ),
        name="fetch_first_kernel",
    )(first_weights, ids)
    arrived, ids, early = lax.optimization_barrier((exchange(partial), ids, early))
    partial, upper = pl.pallas_call(
        first_section,
        in_specs=[near, near, near, near],
        out_specs=[far, near],
        out_shape=[sums_shape, upper_shape],
        scratch_shapes=scratch,
        compiler_params=params,
        cost_estimate=cost,
        name="first_section",
    )(arrived, grad, first, early)
    ids = lax.optimization_barrier((ids, partial))[0]
    ids = lax.psum(ids, "trial", axis_index_groups=quarters)
    arrived, ids = lax.optimization_barrier((exchange(partial), ids))
    flat_shape = (neurons * trials, steps)
    parts = pl.pallas_call(
        readin,
        in_specs=[near, near, near],
        out_specs=far,
        out_shape=pltpu.HBM((neurons * trials, own), jnp.bfloat16),
        scratch_shapes=[
            pltpu.VMEM((sections, neurons * trials // sections, own), jnp.bfloat16),
            pltpu.SemaphoreType.DMA((sections,)),
        ],
        compiler_params=params,
        cost_estimate=pl.CostEstimate(
            flops=2 * neurons * trials * trials * own * steps,
            bytes_accessed=4 * neurons * trials * own,
            transcendentals=0,
        ),
        name="readin",
    )(arrived, upper, spike_rates.reshape(flat_shape))
    parts = parts.reshape(shards, block * trials, own)
    arrived = lax.all_to_all(parts, "trial", split_axis=0, concat_axis=0, tiled=True)
    ids = lax.optimization_barrier((ids, parts))[0]
    ids = lax.psum(ids, "trial", axis_index_groups=neighbours)
    keys = ids.reshape(shards, 1, trials) * block + lax.broadcasted_iota(jnp.int32, (1, block, 1), 1)
    slots = lax.broadcasted_iota(jnp.int32, (shards * block, 1), 0)
    chosen = (keys.reshape(1, -1) == slots).astype(jnp.bfloat16)
    summed = jnp.dot(chosen, arrived.reshape(-1, own), preferred_element_type=jnp.float32)
    return summed.astype(jnp.bfloat16).reshape(shards, block, own)


def solution(mesh):
    in_specs = (
        P(None, "trial", None),
        P("section", "trial", None),
        P("section", "trial", None),
        P("section", "trial", None),
        P(None, None, "section"),
        P(None, None, "section"),
        P("trial"),
    )
    out_specs = P(None, "trial", "section")
    return jax.shard_map(body, mesh=mesh, in_specs=in_specs, out_specs=out_specs, check_vma=False)
```
